256 devices in a mesh: samp: 8 (over z), arow: 4 (over y), acol: 8 (over x, core).
Axes of the slice: x: 4, y: 4, z: 8, core: 2. Of those that a mesh axis runs over, the one named last changes fastest.
Arguments:
- embeddings: bfloat16 [393216, 768], P(('samp', 'arow', 'acol')), may hold values from -6 to 6
- anchors: bfloat16 [65536, 768], P(('arow', 'acol')), may hold values from -6 to 6
- subspace: bfloat16 [65536, 64], P(('arow', 'acol')), may hold values from -3 to 3
- nearest: int32 [393216, 8], P(('samp', 'arow', 'acol')), may hold values from 0 to 65535, as said below
Outputs:
- gram_product: float32 [65536, 64], P(('arow', 'acol'))
The draws below stay inside these ranges and needn't reach their ends.
Inputs may be any that keep to these rules, and one draw needn't show every extreme that they name: `nearest`: anchor shard o holds anchors 2048 * o to 2048 * (o + 1) - 1. The rows of one device name anchors of every one of the 32 shards, and within each of them only anchors of one aligned block of 128. The 8 anchors of a row are distinct.
All inputs are finite; a program needn't handle non-finite values.
Results may differ from the reference program's by a relative error of at most 0.0003.
Values may be sent and summed in bfloat16 or wider, within the bound.
A program may use at most 128 MiB of HBM per device.

```python
import jax
import jax.numpy as jnp
from jax import lax

D = 768
COLS = 64
CAND = 8
ANC_DEV = 2048
BA = 128
ROW_DEV = 1536
OWNERS = 32
USED = 32
ANCHORS = 65536
ROWS = 393216
DEVICES = 256


def draw_nearest(key, part):
    span = USED * BA
    spacing = span // CAND
    key_order = jax.random.fold_in(key, 11)
    key_pick = jax.random.fold_in(key, 23)
    key_base = jax.random.fold_in(key, 37)
    key_jitter = jax.random.fold_in(key, 41)
    orders = jax.vmap(lambda sub_key: jax.random.permutation(sub_key, OWNERS))(jax.random.split(key_order, DEVICES))
    users = orders[:, :USED]
    picks = jax.random.randint(key_pick, (DEVICES, OWNERS), 0, ANC_DEV // BA)
    row_index = jnp.arange(ROW_DEV, dtype=jnp.int32)
    base = (row_index % USED)[None, :] * BA + jax.random.randint(key_base, (DEVICES, ROW_DEV), 0, BA)
    jitter = jax.random.randint(key_jitter, (DEVICES, ROW_DEV, CAND), 0, spacing)
    jitter = jitter * (jnp.arange(CAND, dtype=jnp.int32) > 0).astype(jnp.int32)
    places = (base[:, :, None] + jnp.arange(CAND, dtype=jnp.int32) * spacing + jitter) % span
    owner_pick = jnp.take_along_axis(users, (places // BA).reshape(DEVICES, -1), axis=1)
    block_pick = jnp.take_along_axis(picks, owner_pick, axis=1)
    anchor_ids = owner_pick * ANC_DEV + block_pick * BA + (places % BA).reshape(DEVICES, -1)
    return anchor_ids.reshape(DEVICES * ROW_DEV, CAND).astype(jnp.int32)


def block_levels(key, dims, cuts, smallest, top_value):
    factor_of, own = 1.0, jax.random.fold_in(key, 6)
    for axis_at, blocks in cuts:
        steps = jnp.exp(jax.random.uniform(jax.random.fold_in(own, axis_at), (blocks,), jnp.float32, smallest / len(cuts), top_value / len(cuts)))
        factor_of = factor_of * jnp.repeat(steps, dims[axis_at] // blocks).reshape([-1 if axis == axis_at else 1 for axis in range(len(dims))])
    return factor_of


def scatter_about(rng, shape, deviation, bound, cuts=(), held_as=jnp.bfloat16):
    values = deviation * jax.random.normal(rng, shape, jnp.float32)
    if cuts:
        values = values * block_levels(rng, shape, cuts, -0.22, 0.18)
    return jnp.clip(values, -bound, bound).astype(held_as)


def setup_inputs(seed: int = 0) -> dict:
    splits = jax.random.split(jax.random.key(seed), 5)
    return {
        "embeddings": scatter_about(splits[0], (ROWS, D), 1.0, 6.0, ((0, 256),)),
        "anchors": scatter_about(splits[1], (ANCHORS, D), 1.0, 6.0, ((0, 32),)),
        "subspace": scatter_about(splits[2], (ANCHORS, COLS), 0.5, 3.0, ((0, 32),)),
        "nearest": draw_nearest(jax.random.fold_in(splits[4], 71), 0),
    }


def reference(embeddings, anchors, subspace, nearest):
    anchor_float = anchors.astype(jnp.float32)
    anchor_scale = lax.rsqrt(lax.optimization_barrier(jnp.mean(anchor_float * anchor_float, axis=1)) + 1e-06)
    row_groups = embeddings.reshape(-1, ROW_DEV, D)
    near_groups = nearest.reshape(-1, ROW_DEV, CAND)

    def accumulate(running, inputs):
        group_rows, group_near = inputs
        rows_float = group_rows.astype(jnp.float32)
        row_scale = lax.rsqrt(lax.optimization_barrier(jnp.mean(rows_float * rows_float, axis=1)) + 1e-06)
        picked = anchor_float[group_near]
        dots = jnp.einsum('rd,rkd->rk', rows_float, picked, precision=lax.Precision.HIGHEST)
        cosine = dots * row_scale[:, None] * anchor_scale[group_near] / D
        kernel = jnp.exp((cosine - 1.0) / 0.05)
        weights = kernel / lax.optimization_barrier(jnp.sum(kernel, axis=1, keepdims=True))
        panel = subspace[group_near].astype(jnp.float32)
        projected = jnp.einsum('rk,rkc->rc', weights, panel, precision=lax.Precision.HIGHEST)
        terms = weights[:, :, None] * projected[:, None, :]
        running = running.at[group_near.reshape(-1)].add(terms.reshape(-1, COLS))
        return (running, None)
    result, _ = lax.scan(accumulate, jnp.zeros((ANCHORS, COLS), jnp.float32), (row_groups, near_groups))
    return result
```

```python
import functools

import jax
import jax.numpy as jnp
from jax import lax
from jax.experimental import pallas as pl
from jax.experimental.pallas import tpu as pltpu
from jax.sharding import PartitionSpec as P

D = 768
COLS = 64
CAND = 8
BA = 128
OWNERS = 32
BLOCKS = 16
ROWS = 1536
PLANES = 8
RC = 256
MESH = pl.DeviceIdType.MESH
SCALE = 20.0 * 1.4426950408889634 / D

ORDER = (
    (0, 0), (0, 1), (1, 0), (0, 3), (3, 0), (0, 2), (2, 0), (1, 1),
    (3, 3), (1, 3), (3, 1), (2, 2), (2, 1), (1, 2), (2, 3), (3, 2),
)


def packed(which):
    word = sum(offset[which] << (2 * t) for t, offset in enumerate(ORDER))
    return word - (1 << 32) if word >= 1 << 31 else word


KY, KX = packed(0), packed(1)


def digit(word, t):
    return lax.shift_right_logical(jnp.int32(word), jnp.int32(2) * t) & 3


def nt(a, b):
    return lax.dot_general(a, b, (((1,), (1,)), ((), ())), preferred_element_type=jnp.float32)


def nn(a, b):
    return lax.dot_general(a, b, (((1,), (0,)), ((), ())), preferred_element_type=jnp.float32)


def kernel(
    emb_hbm, anc_hbm, sub_ref, near_ref, out_ref,
    emb, anc, sub, best, ask, table, table_s, bits_s,
    stage_a, stage_v, slots, panel, panel1, words, rscale, high, low, sums, lhs,
    give, back, acc, part, whole,
    local_sem, table_sem, ask_s, ask_r, anc_s, anc_r, pan_s, pan_r, ret_s, ret_r,
    red_s, red_r, gat_s, gat_r,
):
    z = lax.axis_index("samp")
    y = lax.axis_index("arow")
    a = lax.axis_index("acol")
    x = lax.div(a, 2)
    c = lax.rem(a, 2)
    me = y * 8 + a

    def receiver(t, dc):
        sign = 1 - 2 * c
        py = lax.rem(y + 4 + sign * digit(KY, t), 4)
        px = lax.rem(x + 4 + sign * digit(KX, t), 4)
        return (z, py, px * 2 + lax.rem(c + dc, 2))

    def holder(t, dc):
        core = lax.rem(c + dc, 2)
        sign = 1 - 2 * core
        py = lax.rem(y + 4 - sign * digit(KY, t), 4)
        px = lax.rem(x + 4 - sign * digit(KX, t), 4)
        return (z, py, px * 2 + core)

    emb_copy = pltpu.make_async_copy(emb_hbm, emb, local_sem.at[0])
    anc_copy = pltpu.make_async_copy(anc_hbm, anc, local_sem.at[1])
    anc_copy.start()
    emb_copy.start()

    barrier = pltpu.get_barrier_semaphore()

    @pl.loop(1, OWNERS)
    def _(i):
        p = lax.rem(me + i, OWNERS)
        pl.semaphore_signal(
            barrier, inc=1, device_id=(z, lax.div(p, 8), lax.rem(p, 8)), device_id_type=MESH
        )

    @pl.loop(1, PLANES)
    def _(i):
        pl.semaphore_signal(
            barrier, inc=1, device_id=(lax.rem(z + i, PLANES), y, a), device_id_type=MESH
        )

    near = near_ref[...]
    owner = near >> 11
    block = (near >> 7) & 15
    for o in range(OWNERS):
        m = jnp.where(owner == o, block, 0)
        parts = [m[:, i * 128 : (i + 1) * 128] for i in range(ROWS // 128)]
        while len(parts) > 1:
            parts = [
                jnp.maximum(parts[i], parts[i + 1]) if i + 1 < len(parts) else parts[i]
                for i in range(0, len(parts), 2)
            ]
        best[o : o + 1, :] = jnp.max(parts[0], axis=0, keepdims=True)
    wanted = jnp.broadcast_to(jnp.max(best[...], axis=1, keepdims=True), (OWNERS, 128))
    for o in range(OWNERS):
        ask[o] = wanted[o : o + 1, :]

    pl.semaphore_wait(barrier, OWNERS - 1 + PLANES - 1)

    def ask_copy(t, dc):
        n = 2 * t + dc
        to = holder(t, dc)
        return pltpu.make_async_remote_copy(
            src_ref=ask.at[to[1] * 8 + to[2]], dst_ref=table.at[n],
            send_sem=ask_s.at[n], recv_sem=ask_r.at[n], device_id=to, device_id_type=MESH,
        )

    def anchor_copy(t, dc):
        n = 2 * t + dc
        return pltpu.make_async_remote_copy(
            src_ref=stage_a.at[n], dst_ref=slots.at[t, pl.ds(dc * BA, BA)],
            send_sem=anc_s.at[n], recv_sem=anc_r.at[n],
            device_id=receiver(t, dc), device_id_type=MESH,
        )

    def panel_copy(t, dc):
        n = 2 * t + dc
        return pltpu.make_async_remote_copy(
            src_ref=stage_v.at[n], dst_ref=panel.at[n],
            send_sem=pan_s.at[n], recv_sem=pan_r.at[n],
            device_id=receiver(t, dc), device_id_type=MESH,
        )

    def return_copy(t, dc):
        n = 2 * t + dc
        return pltpu.make_async_remote_copy(
            src_ref=give.at[n], dst_ref=back.at[n],
            send_sem=ret_s.at[n], recv_sem=ret_r.at[n],
            device_id=holder(t, dc), device_id_type=MESH,
        )

    def each(body):
        body(jnp.int32(0), 1)

        @pl.loop(1, 16)
        def _(t):
            body(t, 0)
            body(t, 1)

    each(lambda t, dc: ask_copy(t, dc).start())

    for b in range(BLOCKS):
        sub[b] = sub_ref[:, b * BA : (b + 1) * BA]
    panel1[COLS:, :] = jnp.ones((BA - COLS, 2 * BA), jnp.bfloat16)
    table[0] = ask[me]

    @pl.loop(0, 16)
    def _(t):
        for dc in range(2):
            h = holder(t, dc)
            bits_s[2 * t + dc] = lax.shift_left(jnp.int32(1), h[1] * 8 + h[2])

    anc_copy.wait()
    each(lambda t, dc: ask_copy(t, dc).wait_recv())
    to_scalar = pltpu.make_async_copy(table, table_s, table_sem)
    to_scalar.start()
    to_scalar.wait()

    def stage(t, dc):
        n = 2 * t + dc
        b = table_s[n, 0, 0] & (BLOCKS - 1)
        stage_a[n] = anc[b]
        stage_v[n] = sub[b]
        anchor_copy(t, dc).start()
        panel_copy(t, dc).start()

    each(stage)
    own = table_s[0, 0, 0] & (BLOCKS - 1)
    slots[0, 0:BA, :] = anc[own]
    panel[0] = sub[own]

    place = near & (BA - 1)
    flag = lax.shift_left(jnp.ones_like(owner), owner)
    lane = lax.broadcasted_iota(jnp.int32, (BA, BA), 1)
    for g in range(ROWS // BA):
        place_t = jnp.transpose(place[:, g * BA : (g + 1) * BA])
        flag_t = jnp.transpose(flag[:, g * BA : (g + 1) * BA])
        word = jnp.zeros((BA, BA), jnp.int32)
        for k in range(CAND):
            word = word | jnp.where(lane == place_t[:, k : k + 1], flag_t[:, k : k + 1], 0)
        words[g * BA : (g + 1) * BA, :] = word

    emb_copy.wait()

    @pl.loop(0, ROWS // BA)
    def _(g):
        rows = pl.ds(pl.multiple_of(g * BA, BA), BA)
        e = emb[rows, :].astype(jnp.float32)
        mean = jnp.sum(e * e, axis=1, keepdims=True) * (1.0 / D)
        rscale[rows, :] = jnp.broadcast_to(lax.rsqrt(mean + 1e-6) * SCALE, (BA, BA))

    sums[...] = jnp.zeros_like(sums)

    def pair(t):
        panel1[0:COLS, 0:BA] = panel[2 * t]
        panel1[0:COLS, BA:] = panel[2 * t + 1]
        anchors = slots[t]
        wide = anchors.astype(jnp.float32)
        mean = jnp.sum(wide * wide, axis=1, keepdims=True) * (1.0 / D)
        ascale = jnp.broadcast_to(lax.rsqrt(mean + 1e-6), (2 * BA, BA))
        ascale = jnp.transpose(ascale)[0:1, :]
        bit0 = bits_s[2 * t]
        bit1 = bits_s[2 * t + 1]

        @pl.loop(0, ROWS // RC)
        def _(g):
            rows = pl.ds(pl.multiple_of(g * RC, RC), RC)
            dots = nt(emb[rows, :], slots[t])
            word = words[rows, :]
            rs = rscale[rows, :]
            v1 = panel1[...]
            w0 = jnp.where((word & bit0) != 0, jnp.exp2(dots[:, :BA] * rs * ascale[:, :BA]), 0.0)
            w1 = jnp.where((word & bit1) != 0, jnp.exp2(dots[:, BA:] * rs * ascale[:, BA:]), 0.0)
            w = jnp.concatenate([w0, w1], axis=1)
            hi = w.astype(jnp.bfloat16)
            lo = (w - hi.astype(jnp.float32)).astype(jnp.bfloat16)
            high[t, rows, :] = hi
            low[t, rows, :] = lo
            sums[rows, :] += nt(hi, v1) + nt(lo, v1)

    zero = jnp.int32(0)
    anchor_copy(zero, 1).wait_recv()
    panel_copy(zero, 1).wait_recv()
    pair(zero)

    @pl.loop(1, 16)
    def _(t):
        for dc in range(2):
            anchor_copy(t, dc).wait_recv()
            panel_copy(t, dc).wait_recv()
        pair(t)

    @pl.loop(0, ROWS // BA)
    def _(g):
        rows = pl.ds(pl.multiple_of(g * BA, BA), BA)
        u = sums[rows, :]
        inverse = 1.0 / pltpu.roll(u, COLS, 1)
        proj = jnp.transpose(u * inverse * inverse)[0:COLS, :]
        hi = proj.astype(jnp.bfloat16)
        lhs[0:COLS, rows] = hi
        lhs[COLS:, rows] = (proj - hi.astype(jnp.float32)).astype(jnp.bfloat16)

    def product(t):
        r1 = nn(lhs[...], high[t])
        r2 = nn(lhs[0:COLS, :], low[t])
        return r1[0:COLS, :] + r1[COLS:, :] + r2

    @pl.loop(0, 15)
    def _(i):
        t = 15 - i
        g = product(t)
        for dc in range(2):
            give[2 * t + dc] = g[:, dc * BA : (dc + 1) * BA]
            return_copy(t, dc).start()

    g = product(zero)
    back[0] = g[:, 0:BA]
    give[1] = g[:, BA:]
    return_copy(zero, 1).start()

    acc[...] = jnp.zeros_like(acc)

    def collect(n):
        value = back[n]
        b = table_s[n, 0, 0] & (BLOCKS - 1)
        for i in range(BLOCKS):
            acc[i] += jnp.where(b == i, value, 0.0)

    @pl.loop(0, 15)
    def _(i):
        t = 15 - i
        for dc in range(2):
            return_copy(t, dc).wait_recv()
            collect(2 * t + dc)

    collect(0)
    return_copy(zero, 1).wait_recv()
    collect(1)

    def reduce_copy(k):
        to = lax.rem(z + k, PLANES)
        return pltpu.make_async_remote_copy(
            src_ref=acc.at[pl.ds(2 * to, 2)], dst_ref=part.at[k],
            send_sem=red_s.at[k], recv_sem=red_r.at[k],
            device_id=(to, y, a), device_id_type=MESH,
        )

    def gather_copy(k):
        to = lax.rem(z + k, PLANES)
        return pltpu.make_async_remote_copy(
            src_ref=whole.at[pl.ds(2 * z, 2)], dst_ref=whole.at[pl.ds(2 * z, 2)],
            send_sem=gat_s.at[k], recv_sem=gat_r.at[k],
            device_id=(to, y, a), device_id_type=MESH,
        )

    for k in (4, 3, 5, 2, 6, 1, 7):
        reduce_copy(k).start()
    total = acc[pl.ds(2 * z, 2)]
    for k in (1, 7, 2, 6, 3, 5, 4):
        reduce_copy(k).wait_recv()
        total = total + part[k]
    whole[pl.ds(2 * z, 2)] = total
    for k in (4, 3, 5, 2, 6, 1, 7):
        gather_copy(k).start()
    for k in range(1, PLANES):
        gather_copy(k).wait_recv()
    for b in range(BLOCKS):
        out_ref[:, b * BA : (b + 1) * BA] = whole[b]

    @pl.loop(1, PLANES)
    def _(k):
        reduce_copy(k).wait_send()
        gather_copy(k).wait_send()

    def drain(t, dc):
        ask_copy(t, dc).wait_send()
        anchor_copy(t, dc).wait_send()
        panel_copy(t, dc).wait_send()
        return_copy(t, dc).wait_send()

    each(drain)


def per_device(embeddings, anchors, subspace, nearest):
    dma = pltpu.SemaphoreType.DMA
    bf16, f32, i32 = jnp.bfloat16, jnp.float32, jnp.int32
    out = pl.pallas_call(
        kernel,
        out_shape=jax.ShapeDtypeStruct((COLS, BLOCKS * BA), f32),
        in_specs=[
            pl.BlockSpec(memory_space=pl.ANY),
            pl.BlockSpec(memory_space=pl.ANY),
            pl.BlockSpec(memory_space=pltpu.VMEM),
            pl.BlockSpec(memory_space=pltpu.VMEM),
        ],
        out_specs=pl.BlockSpec(memory_space=pltpu.VMEM),
        scratch_shapes=[
            pltpu.VMEM((ROWS, D), bf16),
            pltpu.VMEM((BLOCKS, BA, D), bf16),
            pltpu.VMEM((BLOCKS, COLS, BA), bf16),
            pltpu.VMEM((OWNERS, 128), i32),
            pltpu.VMEM((OWNERS, 1, 128), i32),
            pltpu.VMEM((OWNERS, 1, 128), i32),
            pltpu.SMEM((OWNERS, 1, 128), i32),
            pltpu.SMEM((OWNERS,), i32),
            pltpu.VMEM((OWNERS, BA, D), bf16),
            pltpu.VMEM((OWNERS, COLS, BA), bf16),
            pltpu.VMEM((16, 2 * BA, D), bf16),
            pltpu.VMEM((OWNERS, COLS, BA), bf16),
            pltpu.VMEM((BA, 2 * BA), bf16),
            pltpu.VMEM((ROWS, BA), i32),
            pltpu.VMEM((ROWS, BA), f32),
            pltpu.VMEM((16, ROWS, 2 * BA), bf16),
            pltpu.VMEM((16, ROWS, 2 * BA), bf16),
            pltpu.VMEM((ROWS, BA), f32),
            pltpu.VMEM((BA, ROWS), bf16),
            pltpu.VMEM((OWNERS, COLS, BA), f32),
            pltpu.VMEM((OWNERS, COLS, BA), f32),
            pltpu.VMEM((BLOCKS, COLS, BA), f32),
            pltpu.VMEM((PLANES, 2, COLS, BA), f32),
            pltpu.VMEM((BLOCKS, COLS, BA), f32),
            dma((2,)),
            dma,
        ]
        + [dma((OWNERS,))] * 8
        + [dma((PLANES,))] * 4,
        compiler_params=pltpu.CompilerParams(
            collective_id=0, has_side_effects=True, vmem_limit_bytes=62 * 1024 * 1024
        ),
    )(embeddings, anchors.reshape(BLOCKS, BA, D), subspace.T, nearest.T)
    return out.T


def solution(mesh):
    in_specs = (
        P(("samp", "arow", "acol"), None),
        P(("arow", "acol"), None),
        P(("arow", "acol"), None),
        P(("samp", "arow", "acol"), None),
    )
    return jax.shard_map(
        per_device, mesh=mesh, in_specs=in_specs, out_specs=P(("arow", "acol"), None),
        check_vma=False,
    )
```

```python
import functools

import jax
import jax.numpy as jnp
from jax import lax
from jax.experimental import pallas as pl
from jax.experimental.pallas import tpu as pltpu
from jax.sharding import PartitionSpec as P

D = 768
COLS = 64
CAND = 8
BA = 128
OWNERS = 32
BLOCKS = 16
ROWS = 1536
PLANES = 8
RC = 768
HOPS = 4
MESH = pl.DeviceIdType.MESH
SCALE = 20.0 * 1.4426950408889634 / D

ORDER = (
    (0, 0), (0, 1), (1, 0), (0, 3), (3, 0), (0, 2), (2, 0), (1, 1),
    (3, 3), (1, 3), (3, 1), (2, 2), (2, 1), (1, 2), (2, 3), (3, 2),
)


def packed(which):
    word = sum(offset[which] << (2 * t) for t, offset in enumerate(ORDER))
    return word - (1 << 32) if word >= 1 << 31 else word


KY, KX = packed(0), packed(1)


def digit(word, t):
    return lax.shift_right_logical(jnp.int32(word), jnp.int32(2) * t) & 3


def nt(a, b):
    return lax.dot_general(a, b, (((1,), (1,)), ((), ())), preferred_element_type=jnp.float32)


def nn(a, b):
    return lax.dot_general(a, b, (((1,), (0,)), ((), ())), preferred_element_type=jnp.float32)


def kernel(
    emb_hbm, anc_hbm, sub_hbm, near_hbm, out_ref,
    near_v, sub_v, emb, anc, sub, best, ask, table, table_s, bits_s,
    stage_a, stage_v, slots, panel, panel1, words, rscale, high, low, sums, lhs,
    give, back, acc, part, whole,
    local_sem, table_sem, ask_s, ask_r, anc_s, anc_r, pan_s, pan_r, ret_s, ret_r,
    red_s, red_r, gat_s, gat_r,
):
    z = lax.axis_index("samp")
    y = lax.axis_index("arow")
    a = lax.axis_index("acol")
    x = lax.div(a, 2)
    c = lax.rem(a, 2)
    me = y * 8 + a

    def receiver(t, dc):
        sign = 1 - 2 * c
        py = lax.rem(y + 4 + sign * digit(KY, t), 4)
        px = lax.rem(x + 4 + sign * digit(KX, t), 4)
        return (z, py, px * 2 + lax.rem(c + dc, 2))

    def holder(t, dc):
        core = lax.rem(c + dc, 2)
        sign = 1 - 2 * core
        py = lax.rem(y + 4 - sign * digit(KY, t), 4)
        px = lax.rem(x + 4 - sign * digit(KX, t), 4)
        return (z, py, px * 2 + core)

    emb_copy = pltpu.make_async_copy(emb_hbm, emb, local_sem.at[0])
    anc_copy = pltpu.make_async_copy(anc_hbm, anc, local_sem.at[1])
    near_copy = pltpu.make_async_copy(near_hbm, near_v, local_sem.at[2])
    sub_copy = pltpu.make_async_copy(sub_hbm, sub_v, local_sem.at[3])
    near_copy.start()
    anc_copy.start()
    sub_copy.start()
    emb_copy.start()

    barrier = pltpu.get_barrier_semaphore()

    @pl.loop(1, OWNERS)
    def _(i):
        p = lax.rem(me + i, OWNERS)
        pl.semaphore_signal(
            barrier, inc=1, device_id=(z, lax.div(p, 8), lax.rem(p, 8)), device_id_type=MESH
        )

    @pl.loop(1, PLANES)
    def _(i):
        pl.semaphore_signal(
            barrier, inc=1, device_id=(lax.rem(z + i, PLANES), y, a), device_id_type=MESH
        )

    near_copy.wait()
    near = near_v[...]
    owner = near >> 11
    block = (near >> 7) & 15
    for o in range(OWNERS):
        m = jnp.where(owner == o, block, 0)
        parts = [m[:, i * 128 : (i + 1) * 128] for i in range(ROWS // 128)]
        while len(parts) > 1:
            parts = [
                jnp.maximum(parts[i], parts[i + 1]) if i + 1 < len(parts) else parts[i]
                for i in range(0, len(parts), 2)
            ]
        best[o : o + 1, :] = jnp.max(parts[0], axis=0, keepdims=True)
    wanted = jnp.broadcast_to(jnp.max(best[...], axis=1, keepdims=True), (OWNERS, 128))
    for o in range(OWNERS):
        ask[o] = wanted[o : o + 1, :]

    pl.semaphore_wait(barrier, OWNERS - 1 + PLANES - 1)

    def ask_copy(t, dc):
        n = 2 * t + dc
        to = holder(t, dc)
        return pltpu.make_async_remote_copy(
            src_ref=ask.at[to[1] * 8 + to[2]], dst_ref=table.at[n],
            send_sem=ask_s.at[n], recv_sem=ask_r.at[n], device_id=to, device_id_type=MESH,
        )

    def anchor_copy(t, dc):
        n = 2 * t + dc
        return pltpu.make_async_remote_copy(
            src_ref=stage_a.at[n], dst_ref=slots.at[t, pl.ds(dc * BA, BA)],
            send_sem=anc_s.at[n], recv_sem=anc_r.at[n],
            device_id=receiver(t, dc), device_id_type=MESH,
        )

    def panel_copy(t, dc):
        n = 2 * t + dc
        return pltpu.make_async_remote_copy(
            src_ref=stage_v.at[n], dst_ref=panel.at[n],
            send_sem=pan_s.at[n], recv_sem=pan_r.at[n],
            device_id=receiver(t, dc), device_id_type=MESH,
        )

    def return_copy(t, dc):
        n = 2 * t + dc
        return pltpu.make_async_remote_copy(
            src_ref=give.at[n], dst_ref=back.at[n],
            send_sem=ret_s.at[n], recv_sem=ret_r.at[n],
            device_id=holder(t, dc), device_id_type=MESH,
        )

    def each(body):
        body(jnp.int32(0), 1)

        @pl.loop(1, 16)
        def _(t):
            body(t, 0)
            body(t, 1)

    each(lambda t, dc: ask_copy(t, dc).start())

    sub_copy.wait()
    for b in range(BLOCKS):
        sub[b] = sub_v[:, b * BA : (b + 1) * BA]
    panel1[COLS:, :] = jnp.ones((BA - COLS, 2 * BA), jnp.bfloat16)
    table[0] = ask[me]

    @pl.loop(0, 16)
    def _(t):
        for dc in range(2):
            h = holder(t, dc)
            bits_s[2 * t + dc] = lax.shift_left(jnp.int32(1), h[1] * 8 + h[2])

    anc_copy.wait()
    each(lambda t, dc: ask_copy(t, dc).wait_recv())
    to_scalar = pltpu.make_async_copy(table, table_s, table_sem)
    to_scalar.start()
    to_scalar.wait()

    def stage(t, dc):
        n = 2 * t + dc
        b = table_s[n, 0, 0] & (BLOCKS - 1)
        stage_a[n] = anc[b]
        stage_v[n] = sub[b]
        anchor_copy(t, dc).start()
        panel_copy(t, dc).start()

    each(stage)
    own = table_s[0, 0, 0] & (BLOCKS - 1)
    slots[0, 0:BA, :] = anc[own]
    panel[0] = sub[own]

    place = near & (BA - 1)
    flag = lax.shift_left(jnp.ones_like(owner), owner)
    lane = lax.broadcasted_iota(jnp.int32, (BA, BA), 1)
    for g in range(ROWS // BA):
        place_t = jnp.transpose(place[:, g * BA : (g + 1) * BA])
        flag_t = jnp.transpose(flag[:, g * BA : (g + 1) * BA])
        word = jnp.zeros((BA, BA), jnp.int32)
        for k in range(CAND):
            word = word | jnp.where(lane == place_t[:, k : k + 1], flag_t[:, k : k + 1], 0)
        words[g * BA : (g + 1) * BA, :] = word

    emb_copy.wait()

    @pl.loop(0, ROWS // BA)
    def _(g):
        rows = pl.ds(pl.multiple_of(g * BA, BA), BA)
        e = emb[rows, :].astype(jnp.float32)
        mean = jnp.sum(e * e, axis=1, keepdims=True) * (1.0 / D)
        rscale[rows, :] = jnp.broadcast_to(lax.rsqrt(mean + 1e-6) * SCALE, (BA, BA))

    sums[...] = jnp.zeros_like(sums)

    def pair(t):
        panel1[0:COLS, 0:BA] = panel[2 * t]
        panel1[0:COLS, BA:] = panel[2 * t + 1]
        anchors = slots[t]
        wide = anchors.astype(jnp.float32)
        mean = jnp.sum(wide * wide, axis=1, keepdims=True) * (1.0 / D)
        ascale = jnp.broadcast_to(lax.rsqrt(mean + 1e-6), (2 * BA, BA))
        ascale = jnp.transpose(ascale)[0:1, :]
        bit0 = bits_s[2 * t]
        bit1 = bits_s[2 * t + 1]

        @pl.loop(0, ROWS // RC)
        def _(g):
            rows = pl.ds(pl.multiple_of(g * RC, RC), RC)
            dots = nt(emb[rows, :], slots[t])
            word = words[rows, :]
            rs = rscale[rows, :]
            v1 = panel1[...]
            w0 = jnp.where((word & bit0) != 0, jnp.exp2(dots[:, :BA] * rs * ascale[:, :BA]), 0.0)
            w1 = jnp.where((word & bit1) != 0, jnp.exp2(dots[:, BA:] * rs * ascale[:, BA:]), 0.0)
            w = jnp.concatenate([w0, w1], axis=1)
            hi = w.astype(jnp.bfloat16)
            lo = (w - hi.astype(jnp.float32)).astype(jnp.bfloat16)
            high[t, rows, :] = hi
            low[t, rows, :] = lo
            sums[rows, :] += nt(hi, v1) + nt(lo, v1)

    zero = jnp.int32(0)
    anchor_copy(zero, 1).wait_recv()
    panel_copy(zero, 1).wait_recv()
    pair(zero)

    @pl.loop(1, 16)
    def _(t):
        for dc in range(2):
            anchor_copy(t, dc).wait_recv()
            panel_copy(t, dc).wait_recv()
        pair(t)

    for g in range(ROWS // BA):
        rows = pl.ds(g * BA, BA)
        u = sums[rows, :]
        inverse = 1.0 / pltpu.roll(u, COLS, 1)
        proj = jnp.transpose(u * inverse * inverse)[0:COLS, :]
        hi = proj.astype(jnp.bfloat16)
        lhs[0:COLS, rows] = hi
        lhs[COLS:, rows] = (proj - hi.astype(jnp.float32)).astype(jnp.bfloat16)

    def product(t):
        r1 = nn(lhs[...], high[t])
        r2 = nn(lhs[0:COLS, :], low[t])
        return r1[0:COLS, :] + r1[COLS:, :] + r2

    @pl.loop(0, 15)
    def _(i):
        t = 15 - i
        g = product(t)
        for dc in range(2):
            give[2 * t + dc] = g[:, dc * BA : (dc + 1) * BA]
            return_copy(t, dc).start()

    g = product(zero)
    back[0] = g[:, 0:BA]
    give[1] = g[:, BA:]
    return_copy(zero, 1).start()

    acc[...] = jnp.zeros_like(acc)

    def collect(n):
        value = back[n]
        b = table_s[n, 0, 0] & (BLOCKS - 1)
        for i in range(BLOCKS):
            acc[i] += jnp.where(b == i, value, 0.0)

    @pl.loop(0, 15)
    def _(i):
        t = 15 - i
        for dc in range(2):
            return_copy(t, dc).wait_recv()
            collect(2 * t + dc)

    collect(0)
    return_copy(zero, 1).wait_recv()
    collect(1)

    half = COLS // 2
    streams = [(p, way) for p in range(4) for way in range(2)]

    def hops(p, way):
        return HOPS if p // 2 == way else HOPS - 1

    def slab(way, distance):
        return lax.rem(z + (PLANES + distance if way == 0 else PLANES - distance), PLANES)

    def reduce_copy(p, way, s):
        to = slab(way, 1)
        of = slab(way, HOPS + 1 - s)
        return pltpu.make_async_remote_copy(
            src_ref=acc.at[2 * of + p // 2, pl.ds(p % 2 * half, half)], dst_ref=part.at[way, p, s - 1],
            send_sem=red_s.at[way, p, s - 1], recv_sem=red_r.at[way, p, s - 1],
            device_id=(to, y, a), device_id_type=MESH,
        )

    def gather_copy(p, way, s):
        to = slab(way, 1)
        where = whole.at[slab(1 - way, s - 1), p]
        return pltpu.make_async_remote_copy(
            src_ref=where, dst_ref=where,
            send_sem=gat_s.at[way, p, s - 1], recv_sem=gat_r.at[way, p, s - 1],
            device_id=(to, y, a), device_id_type=MESH,
        )

    for s in range(1, HOPS + 1):
        for p in range(4):
            ready = []
            for way in range(2):
                first = HOPS + 1 - hops(p, way)
                if s < first:
                    continue
                if s > first:
                    reduce_copy(p, way, s - 1).wait_recv()
                    of = slab(way, HOPS + 1 - s)
                    acc[2 * of + p // 2, p % 2 * half : (p % 2 + 1) * half] += part[way, p, s - 2]
                ready.append(reduce_copy(p, way, s))
            for copy in ready:
                copy.start()
    for p in range(4):
        for way in range(2):
            reduce_copy(p, way, HOPS).wait_recv()
        total = acc[2 * z + p // 2, p % 2 * half : (p % 2 + 1) * half]
        whole[z, p] = total + part[0, p, HOPS - 1] + part[1, p, HOPS - 1]
        for way in range(2):
            gather_copy(p, way, 1).start()
    for s in range(2, HOPS + 1):
        for p, way in streams:
            if s <= hops(p, way):
                gather_copy(p, way, s - 1).wait_recv()
                gather_copy(p, way, s).start()
    for p, way in streams:
        gather_copy(p, way, hops(p, way)).wait_recv()
    for b in range(BLOCKS):
        for h in range(2):
            out_ref[h * half : (h + 1) * half, b * BA : (b + 1) * BA] = whole[b // 2, b % 2 * 2 + h]
    for p, way in streams:
        for s in range(1, hops(p, way) + 1):
            reduce_copy(p, way, HOPS + 1 - s).wait_send()
            gather_copy(p, way, s).wait_send()

    def drain(t, dc):
        ask_copy(t, dc).wait_send()
        anchor_copy(t, dc).wait_send()
        panel_copy(t, dc).wait_send()
        return_copy(t, dc).wait_send()

    each(drain)


def per_device(embeddings, anchors, subspace, nearest):
    dma = pltpu.SemaphoreType.DMA
    bf16, f32, i32 = jnp.bfloat16, jnp.float32, jnp.int32
    out = pl.pallas_call(
        kernel,
        out_shape=jax.ShapeDtypeStruct((COLS, BLOCKS * BA), f32),
        in_specs=[
            pl.BlockSpec(memory_space=pl.ANY),
            pl.BlockSpec(memory_space=pl.ANY),
            pl.BlockSpec(memory_space=pl.ANY),
            pl.BlockSpec(memory_space=pl.ANY),
        ],
        out_specs=pl.BlockSpec(memory_space=pltpu.VMEM),
        scratch_shapes=[
            pltpu.VMEM((CAND, ROWS), i32),
            pltpu.VMEM((COLS, BLOCKS * BA), bf16),
            pltpu.VMEM((ROWS, D), bf16),
            pltpu.VMEM((BLOCKS, BA, D), bf16),
            pltpu.VMEM((BLOCKS, COLS, BA), bf16),
            pltpu.VMEM((OWNERS, 128), i32),
            pltpu.VMEM((OWNERS, 1, 128), i32),
            pltpu.VMEM((OWNERS, 1, 128), i32),
            pltpu.SMEM((OWNERS, 1, 128), i32),
            pltpu.SMEM((OWNERS,), i32),
            pltpu.VMEM((OWNERS, BA, D), bf16),
            pltpu.VMEM((OWNERS, COLS, BA), bf16),
            pltpu.VMEM((16, 2 * BA, D), bf16),
            pltpu.VMEM((OWNERS, COLS, BA), bf16),
            pltpu.VMEM((BA, 2 * BA), bf16),
            pltpu.VMEM((ROWS, BA), i32),
            pltpu.VMEM((ROWS, BA), f32),
            pltpu.VMEM((16, ROWS, 2 * BA), bf16),
            pltpu.VMEM((16, ROWS, 2 * BA), bf16),
            pltpu.VMEM((ROWS, BA), f32),
            pltpu.VMEM((BA, ROWS), bf16),
            pltpu.VMEM((OWNERS, COLS, BA), f32),
            pltpu.VMEM((OWNERS, COLS, BA), f32),
            pltpu.VMEM((BLOCKS, COLS, BA), f32),
            pltpu.VMEM((2, 4, HOPS, COLS // 2, BA), f32),
            pltpu.VMEM((PLANES, 4, COLS // 2, BA), f32),
            dma((4,)),
            dma,
        ]
        + [dma((OWNERS,))] * 8
        + [dma((2, 4, HOPS))] * 4,
        compiler_params=pltpu.CompilerParams(
            collective_id=0, has_side_effects=True, vmem_limit_bytes=67_043_328
        ),
    )(embeddings, anchors.reshape(BLOCKS, BA, D), subspace.T, nearest.T)
    return out.T


def solution(mesh):
    in_specs = (
        P(("samp", "arow", "acol"), None),
        P(("arow", "acol"), None),
        P(("arow", "acol"), None),
        P(("samp", "arow", "acol"), None),
    )
    return jax.shard_map(
        per_device, mesh=mesh, in_specs=in_specs, out_specs=P(("arow", "acol"), None),
        check_vma=False,
    )
```

```python
import functools

import jax
import jax.numpy as jnp
from jax import lax
from jax.experimental import pallas as pl
from jax.experimental.pallas import tpu as pltpu
from jax.sharding import PartitionSpec as P

D = 768
COLS = 64
CAND = 8
BA = 128
OWNERS = 32
BLOCKS = 16
ROWS = 1536
PLANES = 8
RC = 768
MESH = pl.DeviceIdType.MESH
SCALE = 20.0 * 1.4426950408889634 / D

ORDER = (
    (0, 0), (0, 1), (1, 0), (0, 3), (3, 0), (0, 2), (2, 0), (1, 1),
    (3, 3), (1, 3), (3, 1), (2, 2), (2, 1), (1, 2), (2, 3), (3, 2),
)


def packed(which):
    word = sum(offset[which] << (2 * t) for t, offset in enumerate(ORDER))
    return word - (1 << 32) if word >= 1 << 31 else word


KY, KX = packed(0), packed(1)


def digit(word, t):
    return lax.shift_right_logical(jnp.int32(word), jnp.int32(2) * t) & 3


def nt(a, b):
    return lax.dot_general(a, b, (((1,), (1,)), ((), ())), preferred_element_type=jnp.float32)


def nn(a, b):
    return lax.dot_general(a, b, (((1,), (0,)), ((), ())), preferred_element_type=jnp.float32)


def kernel(
    emb_hbm, anc_hbm, sub_hbm, near_hbm, out_hbm,
    near_v, sub_v, emb, anc, sub, best, ask, table, table_s, bits_s,
    stage_a, stage_v, slots, panel, panel1, words, rscale, high, low, sums, lhs,
    give, back, acc, part, whole,
    local_sem, table_sem, ask_s, ask_r, anc_s, anc_r, pan_s, pan_r, ret_s, ret_r,
    red_s, red_r, gat_s, gat_r, out_sem,
):
    z = lax.axis_index("samp")
    y = lax.axis_index("arow")
    a = lax.axis_index("acol")
    x = lax.div(a, 2)
    c = lax.rem(a, 2)
    me = y * 8 + a

    def receiver(t, dc):
        sign = 1 - 2 * c
        py = lax.rem(y + 4 + sign * digit(KY, t), 4)
        px = lax.rem(x + 4 + sign * digit(KX, t), 4)
        return (z, py, px * 2 + lax.rem(c + dc, 2))

    def holder(t, dc):
        core = lax.rem(c + dc, 2)
        sign = 1 - 2 * core
        py = lax.rem(y + 4 - sign * digit(KY, t), 4)
        px = lax.rem(x + 4 - sign * digit(KX, t), 4)
        return (z, py, px * 2 + core)

    emb_copy = pltpu.make_async_copy(emb_hbm, emb, local_sem.at[0])
    anc_copy = pltpu.make_async_copy(anc_hbm, anc, local_sem.at[1])
    near_copy = pltpu.make_async_copy(near_hbm, near_v, local_sem.at[2])
    sub_copy = pltpu.make_async_copy(sub_hbm, sub_v, local_sem.at[3])
    near_copy.start()
    anc_copy.start()
    sub_copy.start()
    emb_copy.start()

    barrier = pltpu.get_barrier_semaphore()

    @pl.loop(1, OWNERS)
    def _(i):
        p = lax.rem(me + i, OWNERS)
        pl.semaphore_signal(
            barrier, inc=1, device_id=(z, lax.div(p, 8), lax.rem(p, 8)), device_id_type=MESH
        )

    @pl.loop(1, PLANES)
    def _(i):
        pl.semaphore_signal(
            barrier, inc=1, device_id=(lax.rem(z + i, PLANES), y, a), device_id_type=MESH
        )

    near_copy.wait()
    near = near_v[...]
    owner = near >> 11
    block = (near >> 7) & 15
    for o in range(OWNERS):
        m = jnp.where(owner == o, block, 0)
        parts = [m[:, i * 128 : (i + 1) * 128] for i in range(ROWS // 128)]
        while len(parts) > 1:
            parts = [
                jnp.maximum(parts[i], parts[i + 1]) if i + 1 < len(parts) else parts[i]
                for i in range(0, len(parts), 2)
            ]
        best[o : o + 1, :] = jnp.max(parts[0], axis=0, keepdims=True)
    wanted = jnp.broadcast_to(jnp.max(best[...], axis=1, keepdims=True), (OWNERS, 128))
    for o in range(OWNERS):
        ask[o] = wanted[o : o + 1, :]

    pl.semaphore_wait(barrier, OWNERS - 1 + PLANES - 1)

    def ask_copy(t, dc):
        n = 2 * t + dc
        to = holder(t, dc)
        return pltpu.make_async_remote_copy(
            src_ref=ask.at[to[1] * 8 + to[2]], dst_ref=table.at[n],
            send_sem=ask_s.at[n], recv_sem=ask_r.at[n], device_id=to, device_id_type=MESH,
        )

    def anchor_copy(t, dc):
        n = 2 * t + dc
        return pltpu.make_async_remote_copy(
            src_ref=stage_a.at[n], dst_ref=slots.at[t, pl.ds(dc * BA, BA)],
            send_sem=anc_s.at[n], recv_sem=anc_r.at[n],
            device_id=receiver(t, dc), device_id_type=MESH,
        )

    def panel_copy(t, dc):
        n = 2 * t + dc
        return pltpu.make_async_remote_copy(
            src_ref=stage_v.at[n], dst_ref=panel.at[n],
            send_sem=pan_s.at[n], recv_sem=pan_r.at[n],
            device_id=receiver(t, dc), device_id_type=MESH,
        )

    def return_copy(t, dc):
        n = 2 * t + dc
        return pltpu.make_async_remote_copy(
            src_ref=give.at[n], dst_ref=back.at[n],
            send_sem=ret_s.at[n], recv_sem=ret_r.at[n],
            device_id=holder(t, dc), device_id_type=MESH,
        )

    def each(body):
        body(jnp.int32(0), 1)

        @pl.loop(1, 16)
        def _(t):
            body(t, 0)
            body(t, 1)

    each(lambda t, dc: ask_copy(t, dc).start())

    sub_copy.wait()
    for b in range(BLOCKS):
        sub[b] = sub_v[:, b * BA : (b + 1) * BA]
    panel1[COLS:, :] = jnp.ones((BA - COLS, 2 * BA), jnp.bfloat16)
    table[0] = ask[me]

    @pl.loop(0, 16)
    def _(t):
        for dc in range(2):
            h = holder(t, dc)
            bits_s[2 * t + dc] = lax.shift_left(jnp.int32(1), h[1] * 8 + h[2])

    anc_copy.wait()
    each(lambda t, dc: ask_copy(t, dc).wait_recv())
    to_scalar = pltpu.make_async_copy(table, table_s, table_sem)
    to_scalar.start()
    to_scalar.wait()

    def stage(t, dc):
        n = 2 * t + dc
        b = table_s[n, 0, 0] & (BLOCKS - 1)
        stage_a[n] = anc[b]
        stage_v[n] = sub[b]
        anchor_copy(t, dc).start()
        panel_copy(t, dc).start()

    each(stage)
    own = table_s[0, 0, 0] & (BLOCKS - 1)
    slots[0, 0:BA, :] = anc[own]
    panel[0] = sub[own]

    place = near & (BA - 1)
    flag = lax.shift_left(jnp.ones_like(owner), owner)
    lane = lax.broadcasted_iota(jnp.int32, (BA, BA), 1)
    for g in range(ROWS // BA):
        place_t = jnp.transpose(place[:, g * BA : (g + 1) * BA])
        flag_t = jnp.transpose(flag[:, g * BA : (g + 1) * BA])
        word = jnp.zeros((BA, BA), jnp.int32)
        for k in range(CAND):
            word = word | jnp.where(lane == place_t[:, k : k + 1], flag_t[:, k : k + 1], 0)
        words[g * BA : (g + 1) * BA, :] = word

    emb_copy.wait()

    @pl.loop(0, ROWS // BA)
    def _(g):
        rows = pl.ds(pl.multiple_of(g * BA, BA), BA)
        e = emb[rows, :].astype(jnp.float32)
        mean = jnp.sum(e * e, axis=1, keepdims=True) * (1.0 / D)
        rscale[rows, :] = jnp.broadcast_to(lax.rsqrt(mean + 1e-6) * SCALE, (BA, BA))

    sums[...] = jnp.zeros_like(sums)

    def pair(t):
        panel1[0:COLS, 0:BA] = panel[2 * t]
        panel1[0:COLS, BA:] = panel[2 * t + 1]
        anchors = slots[t]
        wide = anchors.astype(jnp.float32)
        mean = jnp.sum(wide * wide, axis=1, keepdims=True) * (1.0 / D)
        ascale = jnp.broadcast_to(lax.rsqrt(mean + 1e-6), (2 * BA, BA))
        ascale = jnp.transpose(ascale)[0:1, :]
        bit0 = bits_s[2 * t]
        bit1 = bits_s[2 * t + 1]

        @pl.loop(0, ROWS // RC)
        def _(g):
            rows = pl.ds(pl.multiple_of(g * RC, RC), RC)
            dots = nt(emb[rows, :], slots[t])
            word = words[rows, :]
            rs = rscale[rows, :]
            v1 = panel1[...]
            w0 = jnp.where((word & bit0) != 0, jnp.exp2(dots[:, :BA] * rs * ascale[:, :BA]), 0.0)
            w1 = jnp.where((word & bit1) != 0, jnp.exp2(dots[:, BA:] * rs * ascale[:, BA:]), 0.0)
            w = jnp.concatenate([w0, w1], axis=1)
            hi = w.astype(jnp.bfloat16)
            lo = (w - hi.astype(jnp.float32)).astype(jnp.bfloat16)
            high[t, rows, :] = hi
            low[t, rows, :] = lo
            sums[rows, :] += nt(hi, v1) + nt(lo, v1)

    zero = jnp.int32(0)
    anchor_copy(zero, 1).wait_recv()
    panel_copy(zero, 1).wait_recv()
    pair(zero)

    @pl.loop(1, 16)
    def _(t):
        for dc in range(2):
            anchor_copy(t, dc).wait_recv()
            panel_copy(t, dc).wait_recv()
        pair(t)

    for g in range(ROWS // BA):
        rows = pl.ds(g * BA, BA)
        u = sums[rows, :]
        inverse = 1.0 / pltpu.roll(u, COLS, 1)
        proj = jnp.transpose(u * inverse * inverse)[0:COLS, :]
        hi = proj.astype(jnp.bfloat16)
        lhs[0:COLS, rows] = hi
        lhs[COLS:, rows] = (proj - hi.astype(jnp.float32)).astype(jnp.bfloat16)

    def product(t):
        r1 = nn(lhs[...], high[t])
        r2 = nn(lhs[0:COLS, :], low[t])
        return r1[0:COLS, :] + r1[COLS:, :] + r2

    @pl.loop(0, 15)
    def _(i):
        t = 15 - i
        g = product(t)
        for dc in range(2):
            give[2 * t + dc] = g[:, dc * BA : (dc + 1) * BA]
            return_copy(t, dc).start()

    g = product(zero)
    back[0] = g[:, 0:BA]
    give[1] = g[:, BA:]
    return_copy(zero, 1).start()

    acc[...] = jnp.zeros_like(acc)

    def collect(n):
        value = back[n]
        b = table_s[n, 0, 0] & (BLOCKS - 1)
        for i in range(BLOCKS):
            acc[i] += jnp.where(b == i, value, 0.0)

    @pl.loop(0, 15)
    def _(i):
        t = 15 - i
        for dc in range(2):
            return_copy(t, dc).wait_recv()
            collect(2 * t + dc)

    collect(0)
    return_copy(zero, 1).wait_recv()
    collect(1)

    half = COLS // 2
    streams = [(p, way) for p in range(4) for way in range(2)]

    def slab(way, distance):
        return lax.rem(z + (PLANES + distance if way == 0 else PLANES - distance), PLANES)

    reduce_hops = ((2, 4), (1, 3), (2, 2), (1, 1))

    def reduce_copy(p, way, slot):
        step, of = reduce_hops[slot]
        return pltpu.make_async_remote_copy(
            src_ref=acc.at[2 * slab(way, of) + p // 2, pl.ds(p % 2 * half, half)],
            dst_ref=part.at[way, p, slot],
            send_sem=red_s.at[way, p, slot], recv_sem=red_r.at[way, p, slot],
            device_id=(slab(way, step), y, a), device_id_type=MESH,
        )

    gather_hops = ((1, 0), (2, 0), (1, 2), (2, 2))

    def gather_copy(p, way, slot):
        step, back_to = gather_hops[slot]
        where = whole.at[slab(1 - way, back_to), p]
        return pltpu.make_async_remote_copy(
            src_ref=where, dst_ref=where,
            send_sem=gat_s.at[way, p, slot], recv_sem=gat_r.at[way, p, slot],
            device_id=(slab(way, step), y, a), device_id_type=MESH,
        )

    def result_copy(p, origin):
        lanes = pl.ds(pl.multiple_of((2 * origin + p // 2) * BA, BA), BA)
        return pltpu.make_async_copy(
            whole.at[origin, p], out_hbm.at[pl.ds(p % 2 * half, half), lanes], out_sem.at[origin, p]
        )

    def far(p, way):
        return p // 2 == way

    for p, way in streams:
        if far(p, way):
            reduce_copy(p, way, 0).start()
    for p, way in streams:
        reduce_copy(p, way, 1).start()
    for p, way in streams:
        reduce_copy(p, way, 3).start()
    for p in range(4):
        columns = slice(p % 2 * half, (p % 2 + 1) * half)
        for way in range(2):
            reduce_copy(p, way, 1).wait_recv()
            value = part[way, p, 1]
            if far(p, way):
                reduce_copy(p, way, 0).wait_recv()
                value = value + part[way, p, 0]
            acc[2 * slab(way, 2) + p // 2, columns] += value
        for way in range(2):
            reduce_copy(p, way, 2).start()
    for p in range(4):
        total = acc[2 * z + p // 2, p % 2 * half : (p % 2 + 1) * half]
        for way in range(2):
            reduce_copy(p, way, 3).wait_recv()
            total = total + part[way, p, 3]
        for way in range(2):
            reduce_copy(p, way, 2).wait_recv()
            total = total + part[way, p, 2]
        whole[z, p] = total
        for way in range(2):
            gather_copy(p, way, 1).start()
        for way in range(2):
            gather_copy(p, way, 0).start()
        result_copy(p, z).start()
    for p, way in streams:
        gather_copy(p, way, 1).wait_recv()
        if far(p, way):
            gather_copy(p, way, 3).start()
        gather_copy(p, way, 2).start()
        result_copy(p, slab(1 - way, 2)).start()
    for p, way in streams:
        gather_copy(p, way, 0).wait_recv()
        result_copy(p, slab(1 - way, 1)).start()
    for p, way in streams:
        gather_copy(p, way, 2).wait_recv()
        result_copy(p, slab(1 - way, 3)).start()
        if far(p, way):
            gather_copy(p, way, 3).wait_recv()
            result_copy(p, slab(1 - way, 4)).start()
    for p, way in streams:
        for slot in range(4):
            if slot > 0 or far(p, way):
                reduce_copy(p, way, slot).wait_send()
            if slot < 3 or far(p, way):
                gather_copy(p, way, slot).wait_send()
    for p in range(4):
        for origin in range(PLANES):
            result_copy(p, origin).wait()

    def drain(t, dc):
        ask_copy(t, dc).wait_send()
        anchor_copy(t, dc).wait_send()
        panel_copy(t, dc).wait_send()
        return_copy(t, dc).wait_send()

    each(drain)


def per_device(embeddings, anchors, subspace, nearest):
    dma = pltpu.SemaphoreType.DMA
    bf16, f32, i32 = jnp.bfloat16, jnp.float32, jnp.int32
    out = pl.pallas_call(
        kernel,
        out_shape=jax.ShapeDtypeStruct((COLS, BLOCKS * BA), f32),
        in_specs=[
            pl.BlockSpec(memory_space=pl.ANY),
            pl.BlockSpec(memory_space=pl.ANY),
            pl.BlockSpec(memory_space=pl.ANY),
            pl.BlockSpec(memory_space=pl.ANY),
        ],
        out_specs=pl.BlockSpec(memory_space=pl.ANY),
        scratch_shapes=[
            pltpu.VMEM((CAND, ROWS), i32),
            pltpu.VMEM((COLS, BLOCKS * BA), bf16),
            pltpu.VMEM((ROWS, D), bf16),
            pltpu.VMEM((BLOCKS, BA, D), bf16),
            pltpu.VMEM((BLOCKS, COLS, BA), bf16),
            pltpu.VMEM((OWNERS, 128), i32),
            pltpu.VMEM((OWNERS, 1, 128), i32),
            pltpu.VMEM((OWNERS, 1, 128), i32),
            pltpu.SMEM((OWNERS, 1, 128), i32),
            pltpu.SMEM((OWNERS,), i32),
            pltpu.VMEM((OWNERS, BA, D), bf16),
            pltpu.VMEM((OWNERS, COLS, BA), bf16),
            pltpu.VMEM((16, 2 * BA, D), bf16),
            pltpu.VMEM((OWNERS, COLS, BA), bf16),
            pltpu.VMEM((BA, 2 * BA), bf16),
            pltpu.VMEM((ROWS, BA), i32),
            pltpu.VMEM((ROWS, BA), f32),
            pltpu.VMEM((16, ROWS, 2 * BA), bf16),
            pltpu.VMEM((16, ROWS, 2 * BA), bf16),
            pltpu.VMEM((ROWS, BA), f32),
            pltpu.VMEM((BA, ROWS), bf16),
            pltpu.VMEM((OWNERS, COLS, BA), f32),
            pltpu.VMEM((OWNERS, COLS, BA), f32),
            pltpu.VMEM((BLOCKS, COLS, BA), f32),
            pltpu.VMEM((2, 4, 4, COLS // 2, BA), f32),
            pltpu.VMEM((PLANES, 4, COLS // 2, BA), f32),
            dma((4,)),
            dma,
        ]
        + [dma((OWNERS,))] * 8
        + [dma((2, 4, 4))] * 4
        + [dma((PLANES, 4))],
        compiler_params=pltpu.CompilerParams(
            collective_id=0, has_side_effects=True, vmem_limit_bytes=67_043_328
        ),
    )(embeddings, anchors.reshape(BLOCKS, BA, D), subspace.T, nearest.T)
    return out.T


def solution(mesh):
    in_specs = (
        P(("samp", "arow", "acol"), None),
        P(("arow", "acol"), None),
        P(("arow", "acol"), None),
        P(("samp", "arow", "acol"), None),
    )
    return jax.shard_map(
        per_device, mesh=mesh, in_specs=in_specs, out_specs=P(("arow", "acol"), None),
        check_vma=False,
    )
```

```python
import functools

import jax
import jax.numpy as jnp
from jax import lax
from jax.experimental import pallas as pl
from jax.experimental.pallas import tpu as pltpu
from jax.sharding import PartitionSpec as P

D = 768
COLS = 64
CAND = 8
BA = 128
OWNERS = 32
BLOCKS = 16
ROWS = 1536
PLANES = 8
RC = 768
MESH = pl.DeviceIdType.MESH
SCALE = 20.0 * 1.4426950408889634 / D

ORDER = (
    (0, 0), (0, 1), (1, 0), (0, 3), (3, 0), (0, 2), (2, 0), (1, 1),
    (3, 3), (1, 3), (3, 1), (2, 2), (2, 1), (1, 2), (2, 3), (3, 2),
)


def packed(which):
    word = sum(offset[which] << (2 * t) for t, offset in enumerate(ORDER))
    return word - (1 << 32) if word >= 1 << 31 else word


KY, KX = packed(0), packed(1)


def digit(word, t):
    return lax.shift_right_logical(jnp.int32(word), jnp.int32(2) * t) & 3


def nt(a, b):
    return lax.dot_general(a, b, (((1,), (1,)), ((), ())), preferred_element_type=jnp.float32)


def nn(a, b):
    return lax.dot_general(a, b, (((1,), (0,)), ((), ())), preferred_element_type=jnp.float32)


def kernel(
    emb_hbm, anc_hbm, sub_hbm, near_hbm, out_hbm,
    near_v, sub_v, emb, anc, sub, best, ask, table, table_s, bits_s,
    stage_a, stage_v, slots, panel, panel1, words, rscale, high, low, sums, lhs,
    give, back, acc, part, whole,
    local_sem, table_sem, ask_s, ask_r, anc_s, anc_r, pan_s, pan_r, ret_s, ret_r,
    red_s, red_r, gat_s, gat_r, out_sem,
):
    z = lax.axis_index("samp")
    y = lax.axis_index("arow")
    a = lax.axis_index("acol")
    x = lax.div(a, 2)
    c = lax.rem(a, 2)
    me = y * 8 + a

    def receiver(t, dc):
        sign = 1 - 2 * c
        py = lax.rem(y + 4 + sign * digit(KY, t), 4)
        px = lax.rem(x + 4 + sign * digit(KX, t), 4)
        return (z, py, px * 2 + lax.rem(c + dc, 2))

    def holder(t, dc):
        core = lax.rem(c + dc, 2)
        sign = 1 - 2 * core
        py = lax.rem(y + 4 - sign * digit(KY, t), 4)
        px = lax.rem(x + 4 - sign * digit(KX, t), 4)
        return (z, py, px * 2 + core)

    emb_copy = pltpu.make_async_copy(emb_hbm, emb, local_sem.at[0])
    anc_copy = pltpu.make_async_copy(anc_hbm, anc, local_sem.at[1])
    near_copy = pltpu.make_async_copy(near_hbm, near_v, local_sem.at[2])
    sub_copy = pltpu.make_async_copy(sub_hbm, sub_v, local_sem.at[3])
    near_copy.start()
    anc_copy.start()
    sub_copy.start()
    emb_copy.start()

    barrier = pltpu.get_barrier_semaphore()

    @pl.loop(1, OWNERS)
    def _(i):
        p = lax.rem(me + i, OWNERS)
        pl.semaphore_signal(
            barrier, inc=1, device_id=(z, lax.div(p, 8), lax.rem(p, 8)), device_id_type=MESH
        )

    @pl.loop(1, PLANES)
    def _(i):
        pl.semaphore_signal(
            barrier, inc=1, device_id=(lax.rem(z + i, PLANES), y, a), device_id_type=MESH
        )

    near_copy.wait()
    near = near_v[...]
    owner = near >> 11
    block = (near >> 7) & 15
    for o in range(OWNERS):
        m = jnp.where(owner == o, block, 0)
        parts = [m[:, i * 128 : (i + 1) * 128] for i in range(ROWS // 128)]
        while len(parts) > 1:
            parts = [
                jnp.maximum(parts[i], parts[i + 1]) if i + 1 < len(parts) else parts[i]
                for i in range(0, len(parts), 2)
            ]
        best[o : o + 1, :] = jnp.max(parts[0], axis=0, keepdims=True)
    wanted = jnp.broadcast_to(jnp.max(best[...], axis=1, keepdims=True), (OWNERS, 128))
    for o in range(OWNERS):
        ask[o] = wanted[o : o + 1, :]

    pl.semaphore_wait(barrier, OWNERS - 1 + PLANES - 1)

    def ask_copy(t, dc):
        n = 2 * t + dc
        to = holder(t, dc)
        return pltpu.make_async_remote_copy(
            src_ref=ask.at[to[1] * 8 + to[2]], dst_ref=table.at[n],
            send_sem=ask_s.at[n], recv_sem=ask_r.at[n], device_id=to, device_id_type=MESH,
        )

    def anchor_copy(t, dc):
        n = 2 * t + dc
        return pltpu.make_async_remote_copy(
            src_ref=stage_a.at[n], dst_ref=slots.at[t, pl.ds(dc * BA, BA)],
            send_sem=anc_s.at[n], recv_sem=anc_r.at[n],
            device_id=receiver(t, dc), device_id_type=MESH,
        )

    def panel_copy(t, dc):
        n = 2 * t + dc
        return pltpu.make_async_remote_copy(
            src_ref=stage_v.at[n], dst_ref=panel.at[n],
            send_sem=pan_s.at[n], recv_sem=pan_r.at[n],
            device_id=receiver(t, dc), device_id_type=MESH,
        )

    def return_copy(t, dc):
        n = 2 * t + dc
        return pltpu.make_async_remote_copy(
            src_ref=give.at[n], dst_ref=back.at[n],
            send_sem=ret_s.at[n], recv_sem=ret_r.at[n],
            device_id=holder(t, dc), device_id_type=MESH,
        )

    def each(body):
        body(jnp.int32(0), 1)

        @pl.loop(1, 16)
        def _(t):
            body(t, 0)
            body(t, 1)

    each(lambda t, dc: ask_copy(t, dc).start())

    sub_copy.wait()
    for b in range(BLOCKS):
        sub[b] = sub_v[:, b * BA : (b + 1) * BA]
    panel1[COLS:, :] = jnp.ones((BA - COLS, 2 * BA), jnp.bfloat16)
    table[0] = ask[me]

    @pl.loop(0, 16)
    def _(t):
        for dc in range(2):
            h = holder(t, dc)
            bits_s[2 * t + dc] = lax.shift_left(jnp.int32(1), h[1] * 8 + h[2])

    anc_copy.wait()

    def to_scalar(i):
        part_of = pl.ds(16 * i, 16)
        return pltpu.make_async_copy(table.at[part_of], table_s.at[part_of], table_sem.at[i])

    ask_copy(jnp.int32(0), 1).wait_recv()
    for i in range(2):

        @pl.loop(max(1, 8 * i), 8 * i + 8)
        def _(t):
            for dc in range(2):
                ask_copy(t, dc).wait_recv()

        to_scalar(i).start()

    def stage(t, dc):
        n = 2 * t + dc
        b = table_s[n, 0, 0] & (BLOCKS - 1)
        stage_a[n] = anc[b]
        stage_v[n] = sub[b]
        anchor_copy(t, dc).start()
        panel_copy(t, dc).start()

    to_scalar(0).wait()
    stage(jnp.int32(0), 1)
    for i in range(2):

        @pl.loop(max(1, 8 * i), 8 * i + 8)
        def _(t):
            stage(t, 0)
            stage(t, 1)

        if i == 0:
            to_scalar(1).wait()

    own = table_s[0, 0, 0] & (BLOCKS - 1)
    slots[0, 0:BA, :] = anc[own]
    panel[0] = sub[own]

    place = near & (BA - 1)
    flag = lax.shift_left(jnp.ones_like(owner), owner)
    lane = lax.broadcasted_iota(jnp.int32, (BA, BA), 1)
    for g in range(ROWS // BA):
        place_t = jnp.transpose(place[:, g * BA : (g + 1) * BA])
        flag_t = jnp.transpose(flag[:, g * BA : (g + 1) * BA])
        word = jnp.zeros((BA, BA), jnp.int32)
        for k in range(CAND):
            word = word | jnp.where(lane == place_t[:, k : k + 1], flag_t[:, k : k + 1], 0)
        words[g * BA : (g + 1) * BA, :] = word

    emb_copy.wait()

    @pl.loop(0, ROWS // BA)
    def _(g):
        rows = pl.ds(pl.multiple_of(g * BA, BA), BA)
        e = emb[rows, :].astype(jnp.float32)
        mean = jnp.sum(e * e, axis=1, keepdims=True) * (1.0 / D)
        rscale[rows, :] = jnp.broadcast_to(lax.rsqrt(mean + 1e-6) * SCALE, (BA, BA))

    sums[...] = jnp.zeros_like(sums)
    acc[...] = jnp.zeros_like(acc)

    def pair(t):
        panel1[0:COLS, 0:BA] = panel[2 * t]
        panel1[0:COLS, BA:] = panel[2 * t + 1]
        anchors = slots[t]
        wide = anchors.astype(jnp.float32)
        mean = jnp.sum(wide * wide, axis=1, keepdims=True) * (1.0 / D)
        ascale = jnp.broadcast_to(lax.rsqrt(mean + 1e-6), (2 * BA, BA))
        ascale = jnp.transpose(ascale)[0:1, :]
        bit0 = bits_s[2 * t]
        bit1 = bits_s[2 * t + 1]

        @pl.loop(0, ROWS // RC)
        def _(g):
            rows = pl.ds(pl.multiple_of(g * RC, RC), RC)
            dots = nt(emb[rows, :], slots[t])
            word = words[rows, :]
            rs = rscale[rows, :]
            v1 = panel1[...]
            w0 = jnp.where((word & bit0) != 0, jnp.exp2(dots[:, :BA] * rs * ascale[:, :BA]), 0.0)
            w1 = jnp.where((word & bit1) != 0, jnp.exp2(dots[:, BA:] * rs * ascale[:, BA:]), 0.0)
            w = jnp.concatenate([w0, w1], axis=1)
            hi = w.astype(jnp.bfloat16)
            lo = (w - hi.astype(jnp.float32)).astype(jnp.bfloat16)
            high[t, rows, :] = hi
            low[t, rows, :] = lo
            sums[rows, :] += nt(hi, v1) + nt(lo, v1)

    zero = jnp.int32(0)
    anchor_copy(zero, 1).wait_recv()
    panel_copy(zero, 1).wait_recv()
    pair(zero)

    @pl.loop(1, 16)
    def _(t):
        for dc in range(2):
            anchor_copy(t, dc).wait_recv()
            panel_copy(t, dc).wait_recv()
        pair(t)

    for g in range(ROWS // BA):
        rows = pl.ds(g * BA, BA)
        u = sums[rows, :]
        inverse = 1.0 / pltpu.roll(u, COLS, 1)
        proj = jnp.transpose(u * inverse * inverse)[0:COLS, :]
        hi = proj.astype(jnp.bfloat16)
        lhs[0:COLS, rows] = hi
        lhs[COLS:, rows] = (proj - hi.astype(jnp.float32)).astype(jnp.bfloat16)

    def product(t):
        r1 = nn(lhs[...], high[t])
        r2 = nn(lhs[0:COLS, :], low[t])
        return r1[0:COLS, :] + r1[COLS:, :] + r2

    @pl.loop(0, 15)
    def _(i):
        t = 15 - i
        g = product(t)
        for dc in range(2):
            give[2 * t + dc] = g[:, dc * BA : (dc + 1) * BA]
            return_copy(t, dc).start()

    g = product(zero)
    back[0] = g[:, 0:BA]
    give[1] = g[:, BA:]
    return_copy(zero, 1).start()

    def drain(t, dc):
        ask_copy(t, dc).wait_send()
        anchor_copy(t, dc).wait_send()
        panel_copy(t, dc).wait_send()

    each(drain)

    def collect(n):
        value = back[n]
        b = table_s[n, 0, 0] & (BLOCKS - 1)
        for i in range(BLOCKS):
            acc[i] += jnp.where(b == i, value, 0.0)

    @pl.loop(0, 15)
    def _(i):
        t = 15 - i
        for dc in range(2):
            return_copy(t, dc).wait_recv()
            collect(2 * t + dc)

    collect(0)
    return_copy(zero, 1).wait_recv()
    collect(1)

    half = COLS // 2
    streams = [(p, way) for p in range(4) for way in range(2)]

    def slab(way, distance):
        return lax.rem(z + (PLANES + distance if way == 0 else PLANES - distance), PLANES)

    reduce_hops = ((2, 4), (1, 3), (2, 2), (1, 1))

    def reduce_copy(p, way, slot):
        step, of = reduce_hops[slot]
        return pltpu.make_async_remote_copy(
            src_ref=acc.at[2 * slab(way, of) + p // 2, pl.ds(p % 2 * half, half)],
            dst_ref=part.at[way, p, slot],
            send_sem=red_s.at[way, p, slot], recv_sem=red_r.at[way, p, slot],
            device_id=(slab(way, step), y, a), device_id_type=MESH,
        )

    gather_hops = ((1, 0), (2, 0), (1, 2), (2, 2))

    def gather_copy(p, way, slot):
        step, back_to = gather_hops[slot]
        where = whole.at[slab(1 - way, back_to), p]
        return pltpu.make_async_remote_copy(
            src_ref=where, dst_ref=where,
            send_sem=gat_s.at[way, p, slot], recv_sem=gat_r.at[way, p, slot],
            device_id=(slab(way, step), y, a), device_id_type=MESH,
        )

    def result_copy(p, origin):
        lanes = pl.ds(pl.multiple_of((2 * origin + p // 2) * BA, BA), BA)
        return pltpu.make_async_copy(
            whole.at[origin, p], out_hbm.at[pl.ds(p % 2 * half, half), lanes], out_sem.at[origin, p]
        )

    def far(p, way):
        return p // 2 == way

    for p, way in streams:
        if far(p, way):
            reduce_copy(p, way, 0).start()
    for p, way in streams:
        reduce_copy(p, way, 1).start()
    for p, way in streams:
        reduce_copy(p, way, 3).start()
    for p in range(4):
        columns = slice(p % 2 * half, (p % 2 + 1) * half)
        for way in range(2):
            reduce_copy(p, way, 1).wait_recv()
            value = part[way, p, 1]
            if far(p, way):
                reduce_copy(p, way, 0).wait_recv()
                value = value + part[way, p, 0]
            acc[2 * slab(way, 2) + p // 2, columns] += value
        for way in range(2):
            reduce_copy(p, way, 2).start()
    for p in range(4):
        total = acc[2 * z + p // 2, p % 2 * half : (p % 2 + 1) * half]
        for way in range(2):
            reduce_copy(p, way, 3).wait_recv()
            total = total + part[way, p, 3]
        for way in range(2):
            reduce_copy(p, way, 2).wait_recv()
            total = total + part[way, p, 2]
        whole[z, p] = total
        for way in range(2):
            gather_copy(p, way, 1).start()
        for way in range(2):
            gather_copy(p, way, 0).start()
        result_copy(p, z).start()
    for p, way in streams:
        gather_copy(p, way, 1).wait_recv()
        if far(p, way):
            gather_copy(p, way, 3).start()
        gather_copy(p, way, 2).start()
        result_copy(p, slab(1 - way, 2)).start()
    for p, way in streams:
        gather_copy(p, way, 0).wait_recv()
        result_copy(p, slab(1 - way, 1)).start()
    for p, way in streams:
        gather_copy(p, way, 2).wait_recv()
        result_copy(p, slab(1 - way, 3)).start()
        if far(p, way):
            gather_copy(p, way, 3).wait_recv()
            result_copy(p, slab(1 - way, 4)).start()
    for p, way in streams:
        for slot in range(4):
            if slot > 0 or far(p, way):
                reduce_copy(p, way, slot).wait_send()
            if slot < 3 or far(p, way):
                gather_copy(p, way, slot).wait_send()
    for p in range(4):
        for origin in range(PLANES):
            result_copy(p, origin).wait()

    each(lambda t, dc: return_copy(t, dc).wait_send())


def per_device(embeddings, anchors, subspace, nearest):
    dma = pltpu.SemaphoreType.DMA
    bf16, f32, i32 = jnp.bfloat16, jnp.float32, jnp.int32
    out = pl.pallas_call(
        kernel,
        out_shape=jax.ShapeDtypeStruct((COLS, BLOCKS * BA), f32),
        in_specs=[
            pl.BlockSpec(memory_space=pl.ANY),
            pl.BlockSpec(memory_space=pl.ANY),
            pl.BlockSpec(memory_space=pl.ANY),
            pl.BlockSpec(memory_space=pl.ANY),
        ],
        out_specs=pl.BlockSpec(memory_space=pl.ANY),
        scratch_shapes=[
            pltpu.VMEM((CAND, ROWS), i32),
            pltpu.VMEM((COLS, BLOCKS * BA), bf16),
            pltpu.VMEM((ROWS, D), bf16),
            pltpu.VMEM((BLOCKS, BA, D), bf16),
            pltpu.VMEM((BLOCKS, COLS, BA), bf16),
            pltpu.VMEM((OWNERS, 128), i32),
            pltpu.VMEM((OWNERS, 1, 128), i32),
            pltpu.VMEM((OWNERS, 1, 128), i32),
            pltpu.SMEM((OWNERS, 1, 128), i32),
            pltpu.SMEM((OWNERS,), i32),
            pltpu.VMEM((OWNERS, BA, D), bf16),
            pltpu.VMEM((OWNERS, COLS, BA), bf16),
            pltpu.VMEM((16, 2 * BA, D), bf16),
            pltpu.VMEM((OWNERS, COLS, BA), bf16),
            pltpu.VMEM((BA, 2 * BA), bf16),
            pltpu.VMEM((ROWS, BA), i32),
            pltpu.VMEM((ROWS, BA), f32),
            pltpu.VMEM((16, ROWS, 2 * BA), bf16),
            pltpu.VMEM((16, ROWS, 2 * BA), bf16),
            pltpu.VMEM((ROWS, BA), f32),
            pltpu.VMEM((BA, ROWS), bf16),
            pltpu.VMEM((OWNERS, COLS, BA), f32),
            pltpu.VMEM((OWNERS, COLS, BA), f32),
            pltpu.VMEM((BLOCKS, COLS, BA), f32),
            pltpu.VMEM((2, 4, 4, COLS // 2, BA), f32),
            pltpu.VMEM((PLANES, 4, COLS // 2, BA), f32),
            dma((4,)),
            dma((2,)),
        ]
        + [dma((OWNERS,))] * 8
        + [dma((2, 4, 4))] * 4
        + [dma((PLANES, 4))],
        compiler_params=pltpu.CompilerParams(
            collective_id=0, has_side_effects=True, vmem_limit_bytes=67_043_328
        ),
    )(embeddings, anchors.reshape(BLOCKS, BA, D), subspace.T, nearest.T)
    return out.T


def solution(mesh):
    in_specs = (
        P(("samp", "arow", "acol"), None),
        P(("arow", "acol"), None),
        P(("arow", "acol"), None),
        P(("samp", "arow", "acol"), None),
    )
    return jax.shard_map(
        per_device, mesh=mesh, in_specs=in_specs, out_specs=P(("arow", "acol"), None),
        check_vma=False,
    )
```
